32 devices in a mesh: groups: 2 (over y), seq: 4 (over z), head: 4 (over x, core).
Axes of the slice: x: 2, y: 2, z: 4, core: 2. Of those that a mesh axis runs over, the one named last changes fastest.
Arguments:
- tokens: bfloat16 [8192, 2048], P(('groups', 'seq'), 'head'), parts along dimension 0, may hold values from -6 to 6
- q_weight: bfloat16 [2048, 2048], P(None, 'head'), may hold values from -0.125 to 0.125
- k_weight: bfloat16 [2048, 2048], P(None, 'head'), may hold values from -0.125 to 0.125
- v_weight: bfloat16 [2048, 2048], P(None, 'head'), may hold values from -0.125 to 0.125
- level_table: float32 [16, 16], P('head'), may hold values from 0.1 to 1
- level_index: int32 [6, 8192], P(None, ('groups', 'seq')), parts along dimension 1, may hold values from 0 to 15
- out_gain: float32 [2048], P('head'), may hold values from 0.5 to 1.5
Outputs:
- attended: bfloat16 [8192, 2048], P(('groups', 'seq'), 'head'), parts along dimension 0
The draws below stay inside these ranges and needn't reach their ends.
There are 2 independent parts, one for each index of `groups`. The reference program is written for one: setup_inputs(seed, part) draws one part's arguments, and reference() takes and returns one part's arrays. A program takes and returns all parts, laid end to end along the dimension named above; an argument that names none is the same for every part. Nothing has to cross between parts.
Inputs may be any that keep to these rules, and one draw needn't show every extreme that they name: `level_index`: row 0 weights a token's own block, row l + 1 its level-l merged state.
All inputs are finite; a program needn't handle non-finite values.
Results may differ from the reference program's by a relative error of at most 0.012.
Values may be sent and summed in bfloat16 or wider, within the bound.
A program may use at most 64 MiB of HBM per device.

```python
import math
import jax
import jax.numpy as jnp
from jax import lax

D = 2048
HEADS = 16
HD = 128
TOK_DEV = 1024
LEVELS = 5
QLEV = 16
TOKENS = 4096
N_SEQ = 4


def set_ends(entries, key, least, largest):
    spot = [jax.random.randint(jax.random.fold_in(key, axis), (), 0, length) for axis, length in enumerate(entries.shape)]
    longest = entries.shape.index(max(entries.shape))
    beside = spot[:longest] + [(spot[longest] + 1) % entries.shape[longest]] + spot[longest + 1:]
    return entries.at[tuple(spot)].set(least).at[tuple(beside)].set(largest)


def block_levels(own_key, extent, split, least, top_value):
    factor_of, own = 1.0, jax.random.fold_in(own_key, 6)
    for dim, blocks in split:
        steps = jnp.exp(jax.random.uniform(jax.random.fold_in(own, dim), (blocks,), jnp.float32, least / len(split), top_value / len(split)))
        factor_of = factor_of * jnp.repeat(steps, extent[dim] // blocks).reshape([-1 if axis == dim else 1 for axis in range(len(extent))])
    return factor_of


def noise(key, extent, spread, limit, cuts=(), kind=jnp.bfloat16):
    result = jax.random.normal(key, extent, jnp.float32) * spread
    if len(cuts) > 0:
        result = block_levels(key, extent, cuts, -0.22, 0.18) * result
    return jnp.clip(result, min=-limit, max=limit).astype(kind)


def setup_inputs(seed: int = 0, part: int = 0) -> dict:
    splits = jax.random.split(jax.random.key(seed), 8)
    part_splits = jax.random.split(jax.random.fold_in(splits[7], part), 8)
    tokens = noise(part_splits[0], (TOKENS, D), 1.0, 6.0, ((0, 4), (1, 4)))
    q_weight = noise(splits[1], (D, HEADS * HD), D ** -0.5, 0.125, ((1, 4),))
    k_weight = noise(splits[2], (D, HEADS * HD), D ** -0.5, 0.125, ((1, 4),))
    v_weight = noise(splits[3], (D, HEADS * HD), D ** -0.5, 0.125, ((1, 4),))
    level_table = jnp.clip(jnp.exp(math.log(1.0) - 2.3025851 * jax.random.uniform(splits[4], (HEADS, QLEV), jnp.float32) ** block_levels(splits[4], (HEADS, QLEV), ((0, 4),), -0.2, 0.2)), 0.1, 1.0)
    level_index = set_ends(jax.random.randint(part_splits[5], (LEVELS + 1, TOKENS), 0, QLEV), jax.random.fold_in(part_splits[5], 1), 0, QLEV - 1).astype(jnp.int32)
    out_gain = jnp.clip(1.0 + 0.1 * jax.random.normal(splits[6], (HEADS * HD,), jnp.float32), 0.5, 1.5)
    return {"tokens": tokens, "q_weight": q_weight, "k_weight": k_weight, "v_weight": v_weight, "level_table": level_table, "level_index": level_index, "out_gain": out_gain}


def unit_norm(raw_rows):
    return (raw_rows / jnp.sqrt(lax.optimization_barrier(jnp.sum(raw_rows * raw_rows, -1, keepdims=True)) + 1e-06)).astype(jnp.bfloat16)

def reference(tokens, q_weight, k_weight, v_weight, level_table, level_index, out_gain):

    def project(weight):
        return jnp.dot(tokens, weight, preferred_element_type=jnp.float32).reshape(TOKENS, HEADS, HD)
    queries = unit_norm(project(q_weight)).reshape(N_SEQ, TOK_DEV, HEADS, HD)
    key_rows = unit_norm(project(k_weight)).reshape(N_SEQ, TOK_DEV, HEADS, HD)
    values = project(v_weight).astype(jnp.bfloat16).reshape(N_SEQ, TOK_DEV, HEADS, HD)
    kv_state = jnp.einsum('bthd,bthe->bhde', key_rows.astype(jnp.float32), values.astype(jnp.float32))
    one_hot = (level_index[:, :, None] == jnp.arange(QLEV, dtype=jnp.int32)[None, None, :]).astype(jnp.float32)
    level_weight = jnp.einsum('ltq,hq->lth', one_hot, level_table, precision=lax.Precision.HIGHEST)
    level_weight = level_weight.reshape(LEVELS + 1, N_SEQ, TOK_DEV, HEADS).transpose(1, 0, 2, 3)
    block_ids = jnp.arange(N_SEQ, dtype=jnp.int32)
    level_span = (2 ** jnp.arange(LEVELS, dtype=jnp.int32)).astype(jnp.int32)
    causal = jnp.arange(TOK_DEV)[:, None] >= jnp.arange(TOK_DEV)[None, :]
    gain_rows = out_gain.reshape(HEADS, HD)

    def one_block(inputs):
        block_q, block_k, block_v, weights_here, block_id = inputs
        scores = jnp.einsum('thd,shd->hts', block_q.astype(jnp.float32), block_k.astype(jnp.float32))
        scores = jnp.where(causal[None], scores, 0.0).astype(jnp.bfloat16)
        local_term = jnp.einsum('hts,shd->thd', scores.astype(jnp.float32), block_v.astype(jnp.float32))
        low_edge = block_id // (2 * level_span) * (2 * level_span)
        high_edge = block_id // level_span * level_span
        membership = ((block_ids[None, :] >= low_edge[:, None]) & (block_ids[None, :] < high_edge[:, None])).astype(jnp.float32)
        merged = jnp.einsum('lc,chde->lhde', membership, kv_state, precision=lax.Precision.HIGHEST)
        scaled = block_q.astype(jnp.float32)[None] * weights_here[1:, :, :, None]
        far_term = jnp.einsum('lthd,lhde->the', scaled, merged, precision=lax.Precision.HIGHEST)
        combined = weights_here[0][:, :, None] * local_term + far_term
        normalized = combined / jnp.sqrt(lax.optimization_barrier(jnp.mean(combined * combined, -1, keepdims=True)) + 1e-06) * gain_rows
        return normalized.astype(jnp.bfloat16)
    attended = lax.map(one_block, (queries, key_rows, values, level_weight, block_ids))
    return attended.reshape(TOKENS, HEADS * HD)
```

```python
import functools

import jax
import jax.numpy as jnp
from jax import lax
from jax.experimental import pallas as pl
from jax.experimental.pallas import tpu as pltpu
from jax.sharding import PartitionSpec as P

MESH = pl.DeviceIdType.MESH
F32 = jnp.float32
BF16 = jnp.bfloat16
EPS = 1e-06
SHARES = (8, 8, 4, 2, 2, 4, 3, 1)
CHUNKS = (1, 1, 3, 1, 2)
AIDED = (2, 3)
GROUPS = (1, 1, 1, 2)
DUAL = 1
CUTS = 2


def row_chunks(rows):
    sizes = [rows // sum(SHARES) * part for part in SHARES]
    starts, at = [], 0
    for size in sizes:
        starts.append((at, size))
        at += size
    return starts


def fused(
    n_head, n_seq, depth,
    tok, wq_in, wk_in, wv_in, table_in, index_in, gain_in,
    out,
    gat, wq, wk, wv, acc_q, acc_k, acc_v, local, scaled_q, lev, state, merged, outbox,
    keys, vals, prior, guests,
    index, gain, table, wide, parts,
    load_sem, near_send, far_send, relay_send, recv_sem, up_send, pass_send, up_recv, aid_send, aid_recv, back_send,
):
    rows, feats = tok.shape
    width = wq_in.shape[1]
    heads, quant = table.shape
    hd = width // heads
    part_rows = hd // CUTS
    pieces = row_chunks(rows)
    relayed = len(pieces) - DUAL
    parts_of, spans, chunks, firsts = [], [], [], []
    for n in CHUNKS:
        first = sum(map(len, parts_of))
        parts_of.append(list(range(first, first + n)))
        chunks.append((pieces[first][0], sum(size for _, size in pieces[first:first + n])))
    for n in GROUPS:
        first = sum(GROUPS[:len(firsts)])
        firsts.append(first)
        spans.append((chunks[first][0], sum(chunks[first + n - 1])))
    me = lax.axis_index("head")
    block = lax.axis_index("seq")
    pair = me // 2
    side = me % 2
    partner = pair * 2 + 1 - side
    n_pair = n_head // 2
    far_pairs = [(pair + 1 + j) % n_pair for j in range(n_pair - 1)]
    aided = AIDED if n_pair == 2 and n_seq > 1 else ()

    def is_aided(n, b):
        if n == AIDED[0]:
            return (b >= 0) & (b < n_seq - 1)
        return b == n_seq - 2

    def cols_of(s):
        return pl.ds(pl.multiple_of(s * feats, feats), feats)

    def wrows(p):
        return pl.ds(pl.multiple_of(p * (2 * feats), 2 * feats), 2 * feats)

    def wpart(p, s):
        return pl.ds(pl.multiple_of((p * 2 + s) * feats, feats), feats)

    loads = [
        pltpu.make_async_copy(tok, gat.at[pair, :, cols_of(side)], load_sem.at[0]),
        pltpu.make_async_copy(wk_in, wk, load_sem.at[1]),
        pltpu.make_async_copy(wv_in, wv, load_sem.at[2]),
        pltpu.make_async_copy(wq_in, wq, load_sem.at[3]),
        pltpu.make_async_copy(index_in, index, load_sem.at[4]),
        pltpu.make_async_copy(gain_in, gain, load_sem.at[5]),
        pltpu.make_async_copy(table_in, table, load_sem.at[6]),
    ]
    barrier = pltpu.get_barrier_semaphore()
    for p in far_pairs:
        for s in (side, 1 - side)[:1 + min(DUAL, 1)]:
            pl.semaphore_signal(barrier, inc=1, device_id={"head": p * 2 + s}, device_id_type=MESH)
    pl.semaphore_signal(barrier, inc=1, device_id={"head": partner}, device_id_type=MESH)

    @pl.when(block > 0)
    def _():
        pl.semaphore_signal(barrier, inc=1, device_id={"seq": block - 1}, device_id_type=MESH)

    @pl.when(block < n_seq - 1)
    def _():
        pl.semaphore_signal(barrier, inc=1, device_id={"seq": block + 1}, device_id_type=MESH)

    if aided:
        for b in (block - 1, block + 1):
            @pl.when((b >= 0) & (b < n_seq))
            def _():
                pl.semaphore_signal(
                    barrier, inc=1, device_id={"head": far_pairs[0] * 2 + side, "seq": b}, device_id_type=MESH
                )

    for n in (6, 4, 5, 0, 1, 2, 3):
        loads[n].start()

    beside = (block + n_seq - 1) // n_seq + (2 * n_seq - 2 - block) // n_seq
    pl.semaphore_wait(barrier, 1 + (n_pair - 1) * (1 + min(DUAL, 1)) + beside * (2 if aided else 1))

    def piece(p, s, c):
        at, size = pieces[c]
        return gat.at[p, pl.ds(at, size), cols_of(s)]

    def far_copy(j, c):
        at, size = pieces[c]
        return pltpu.make_async_remote_copy(
            src_ref=tok.at[pl.ds(at, size), :], dst_ref=piece(pair, side, c),
            send_sem=far_send.at[j, c], recv_sem=recv_sem.at[pair, side, c],
            device_id={"head": far_pairs[j] * 2 + side}, device_id_type=MESH,
        )

    def cross_copy(j, c):
        at, size = pieces[c]
        return pltpu.make_async_remote_copy(
            src_ref=tok.at[pl.ds(at, size), :], dst_ref=piece(pair, side, c),
            send_sem=relay_send.at[j, c], recv_sem=recv_sem.at[pair, side, c],
            device_id={"head": far_pairs[j] * 2 + 1 - side}, device_id_type=MESH,
        )

    def spot(n):
        at = sum(pieces[a][1] for a in AIDED[:AIDED.index(n)])
        return guests.at[pl.ds(at, pieces[n][1]), :]

    def aid_copy(n):
        at, size = pieces[n]
        return pltpu.make_async_remote_copy(
            src_ref=tok.at[pl.ds(at, size), :], dst_ref=spot(n),
            send_sem=aid_send.at[AIDED.index(n)], recv_sem=aid_recv.at[AIDED.index(n)],
            device_id={"head": far_pairs[0] * 2 + side, "seq": block + 1}, device_id_type=MESH,
        )

    def back_copy(n):
        return pltpu.make_async_remote_copy(
            src_ref=spot(n), dst_ref=piece(far_pairs[0], side, n),
            send_sem=back_send.at[AIDED.index(n)], recv_sem=recv_sem.at[far_pairs[0], side, n],
            device_id={"seq": block - 1}, device_id_type=MESH,
        )

    def near_copy(c):
        at, size = pieces[c]
        return pltpu.make_async_remote_copy(
            src_ref=tok.at[pl.ds(at, size), :], dst_ref=piece(pair, side, c),
            send_sem=near_send.at[c], recv_sem=recv_sem.at[pair, side, c],
            device_id={"head": partner}, device_id_type=MESH,
        )

    def relay_copy(j, c):
        p = far_pairs[j]
        return pltpu.make_async_remote_copy(
            src_ref=piece(p, side, c), dst_ref=piece(p, side, c),
            send_sem=relay_send.at[j, c], recv_sem=recv_sem.at[p, side, c],
            device_id={"head": partner}, device_id_type=MESH,
        )

    def arrived(p, s, c):
        here = piece(p, s, c)
        pltpu.make_async_remote_copy(
            src_ref=here, dst_ref=here, send_sem=near_send.at[c], recv_sem=recv_sem.at[p, s, c],
            device_id={"head": partner}, device_id_type=MESH,
        ).wait_recv()

    for n in aided:
        @pl.when(is_aided(n, block))
        def _():
            aid_copy(n).start()
    for c in range(len(pieces)):
        for j in range(n_pair - 1):
            if c in aided:
                @pl.when(jnp.logical_not(is_aided(c, block)))
                def _():
                    far_copy(j, c).start()
            else:
                far_copy(j, c).start()
            if c >= relayed:
                cross_copy(j, c).start()
        near_copy(c).start()

    for level in range(depth):
        @pl.when(block // 2**level % 2 == 0)
        def _():
            merged[:, level * hd:(level + 1) * hd, :] = jnp.zeros((heads, hd, hd), BF16)
    state[...] = jnp.zeros_like(state)

    loads[6].wait()
    for q in range(quant):
        for h in range(heads):
            wide[q:q + 1, h * hd:(h + 1) * hd] = jnp.full((1, hd), table[h, q], F32)
    top = wide[...].astype(BF16)
    rest = wide[...] - top.astype(F32)
    mid = rest.astype(BF16)
    low = (rest - mid.astype(F32)).astype(BF16)
    parts[...] = jnp.concatenate([top, mid, low], axis=0)
    loads[4].wait()
    loads[5].wait()

    step = min(rows, 256)
    for level in range(depth + 1):
        for at in range(0, rows, step):
            column = jnp.broadcast_to(index[level:level + 1, at:at + step], (3 * quant, step))
            ids = lax.broadcasted_iota(jnp.int32, (3 * quant, step), 0) % quant
            one_hot = jnp.where(column == ids, 1.0, 0.0).astype(BF16)
            lev[level, at:at + step, :] = lax.dot_general(
                one_hot, parts[...], (((0,), (0,)), ((), ())), preferred_element_type=F32
            )

    loads[0].wait()
    for copy in loads[1:4]:
        copy.wait()
    for c in range(len(pieces)):
        arrived(pair, 1 - side, c)
    for at in range(0, rows, step):
        here = gat[pair, at:at + step, :]
        for acc, w in ((acc_k, wk), (acc_v, wv), (acc_q, wq)):
            acc[at:at + step, :] = jnp.dot(here, w[wrows(pair), :], preferred_element_type=F32)

    def state_part(level, u):
        return pl.ds(level * hd + u * part_rows, part_rows)

    def up_copy(h, u, level):
        return pltpu.make_async_remote_copy(
            src_ref=outbox.at[h, pl.ds(u * part_rows, part_rows), :],
            dst_ref=merged.at[h, state_part(level, u), :],
            send_sem=up_send.at[h, u], recv_sem=up_recv.at[h, level, u],
            device_id={"seq": block + 1}, device_id_type=MESH,
        )

    def pass_copy(h, u, level):
        here = merged.at[h, state_part(level, u), :]
        return pltpu.make_async_remote_copy(
            src_ref=here, dst_ref=here,
            send_sem=pass_send.at[h, level, u], recv_sem=up_recv.at[h, level, u],
            device_id={"seq": block + 1}, device_id_type=MESH,
        )

    def add_far(total, here, w, p):
        return total + jnp.dot(here, w[wrows(p), :], preferred_element_type=F32)

    def take(c):
        for n in parts_of[c]:
            if n < relayed:
                for j, p in enumerate(far_pairs):
                    arrived(p, side, n)
                    relay_copy(j, n).start()

    def add_side(totals, c, s):
        at, size = chunks[c]
        for p in far_pairs:
            here = gat[p, at:at + size, cols_of(s)]
            totals = [
                total + jnp.dot(here, w[wpart(p, s), :], preferred_element_type=F32)
                for total, w in zip(totals, (wk, wv))
            ]
        return totals

    def keys_and_values(c):
        at, size = chunks[c]
        last = c == len(chunks) - 1
        totals = [acc_k[at:at + size, :], acc_v[at:at + size, :]]
        for n in parts_of[c]:
            if n >= relayed:
                for p in far_pairs:
                    arrived(p, side, n)
        if last:
            totals = add_side(totals, c, side)
        for n in parts_of[c]:
            for p in far_pairs:
                arrived(p, 1 - side, n)
        if last:
            totals = add_side(totals, c, 1 - side)
        else:
            for p in far_pairs:
                here = gat[p, at:at + size, :]
                totals = [add_far(total, here, w, p) for total, w in zip(totals, (wk, wv))]
        raw_k, raw_v = totals
        k_of, v_of = [], []
        for h in range(heads):
            cut = slice(h * hd, (h + 1) * hd)
            k = raw_k[:, cut]
            k_of.append((k * lax.rsqrt(jnp.sum(k * k, -1, keepdims=True) + EPS)).astype(BF16))
            v_of.append(raw_v[:, cut].astype(BF16))
        grown = [
            lax.dot_general(k, v, (((0,), (0,)), ((), ())), preferred_element_type=F32)
            for k, v in zip(k_of, v_of)
        ]
        for h in range(heads):
            cut = slice(h * hd, (h + 1) * hd)
            before = state[h]
            if c in firsts:
                prior[firsts.index(c), h] = before.astype(BF16)
            after = before + grown[h]
            state[h] = after
            if last:
                outbox[h] = after.astype(BF16)
        if last and depth > 0:
            @pl.when(block % 2 == 0)
            def _():
                for h in range(heads):
                    for u in range(CUTS):
                        up_copy(h, u, 0).start()
        for h in range(heads):
            cut = slice(h * hd, (h + 1) * hd)
            keys[at:at + size, cut] = k_of[h]
            vals[at:at + size, cut] = v_of[h]

    def queries(g):
        at, end = spans[g]
        size = end - at
        raw_q = acc_q[at:end, :]
        for p in far_pairs:
            raw_q = add_far(raw_q, gat[p, at:end, :], wq, p)
        cuts = [slice(h * hd, (h + 1) * hd) for h in range(heads)]
        own_of = []
        for h, cut in enumerate(cuts):
            q = raw_q[:, cut]
            q = q * lax.rsqrt(jnp.sum(q * q, -1, keepdims=True) + EPS)
            own_of.append((q * lev[0, at:end, cut]).astype(BF16))
            for level in range(depth):
                scaled_q[h, at:end, level * hd:(level + 1) * hd] = (
                    q * lev[level + 1, at:end, cut]
                ).astype(BF16)
        causal = lax.broadcasted_iota(jnp.int32, (size, size), 0) >= lax.broadcasted_iota(
            jnp.int32, (size, size), 1
        )
        scores_of = [
            lax.dot_general(
                own_of[h], keys[at:end, cut], (((1,), (1,)), ((), ())), preferred_element_type=F32
            )
            for h, cut in enumerate(cuts)
        ]
        scores_of = [jnp.where(causal, scores, 0.0).astype(BF16) for scores in scores_of]
        for h, cut in enumerate(cuts):
            local[at:end, cut] = jnp.dot(
                scores_of[h], vals[at:end, cut], preferred_element_type=F32
            ) + jnp.dot(own_of[h], prior[g, h], preferred_element_type=F32)

    for n in aided:
        @pl.when(is_aided(n, block - 1))
        def _():
            aid_copy(n).wait_recv()
            back_copy(n).start()
    take(0)
    for c in range(len(chunks)):
        if c + 1 < len(chunks):
            take(c + 1)
        keys_and_values(c)
        if c + 1 in firsts:
            queries(firsts.index(c + 1) - 1)

    def wait_level(h, level):
        @pl.when(block // 2**level % 2 == 1)
        def _():
            for u in range(CUTS):
                pass_copy(h, u, level).wait_recv()

    def forward(h):
        for level in range(depth):
            for u in range(CUTS):
                @pl.when(block // 2**level % 2 == 1)
                def _():
                    pass_copy(h, u, level).wait_recv()
                if level > 0:
                    @pl.when((block // 2**level % 2 == 1) & (block % 2**level != 2**level - 1))
                    def _():
                        pass_copy(h, u, level).start()

                    @pl.when(block % 2 ** (level + 1) == 2**level - 1)
                    def _():
                        mine = pl.ds(u * part_rows, part_rows)
                        total = state[h, mine, :]
                        for below in range(level):
                            total = total + merged[h, state_part(below, u), :].astype(F32)
                        outbox[h, mine, :] = total.astype(BF16)
                        up_copy(h, u, level).start()

    def last_queries():
        queries(len(spans) - 1)

    def finish(h):
        cut = slice(h * hd, (h + 1) * hd)
        tile = min(rows, 256)
        for at in range(0, rows, tile):
            both = local[at:at + tile, cut]
            if depth > 0:
                both = both + jnp.dot(
                    scaled_q[h, at:at + tile, :], merged[h], preferred_element_type=F32
                )
            scale = lax.rsqrt(jnp.sum(both * both, -1, keepdims=True) * (1.0 / hd) + EPS)
            out[at:at + tile, cut] = (both * scale * gain[:, cut]).astype(BF16)

    if depth > 0:
        @pl.when((block % 2 == 1) & (block < n_seq - 1))
        def _():
            for h in range(heads):
                forward(h)

    last_queries()

    if depth > 0:
        @pl.when((block % 2 == 0) & (block < n_seq - 1))
        def _():
            for h in range(heads):
                forward(h)

    @pl.when(block < n_seq - 1)
    def _():
        for h in range(heads):
            finish(h)

    @pl.when(block == n_seq - 1)
    def _():
        for h in range(heads):
            for level in range(depth):
                wait_level(h, level)
            finish(h)

    for n in aided:
        @pl.when(is_aided(n, block))
        def _():
            aid_copy(n).wait_send()

        @pl.when(is_aided(n, block - 1))
        def _():
            back_copy(n).wait_send()
    for c in range(len(pieces)):
        near_copy(c).wait_send()
        for j in range(n_pair - 1):
            if c in aided:
                @pl.when(jnp.logical_not(is_aided(c, block)))
                def _():
                    far_copy(j, c).wait_send()
            else:
                far_copy(j, c).wait_send()
            (relay_copy if c < relayed else cross_copy)(j, c).wait_send()
    for h in range(heads):
        for u in range(CUTS):
            if depth > 0:
                @pl.when(block < n_seq - 1)
                def _():
                    up_copy(h, u, 0).wait_send()
            for level in range(1, depth):
                @pl.when((block // 2**level % 2 == 1) & (block % 2**level != 2**level - 1))
                def _():
                    pass_copy(h, u, level).wait_send()


def on_device(n_head, n_seq, tokens, q_weight, k_weight, v_weight, level_table, level_index, out_gain):
    rows, feats = tokens.shape
    total, width = q_weight.shape
    heads, quant = level_table.shape
    hd = width // heads
    depth = min(n_seq.bit_length() - 1, level_index.shape[0] - 1)
    pairs = n_head // 2
    far = max(pairs - 1, 1)
    n_chunk = len(SHARES)
    dma = pltpu.SemaphoreType.DMA
    anywhere = pl.BlockSpec(memory_space=pltpu.HBM)
    result = pl.pallas_call(
        functools.partial(fused, n_head, n_seq, depth),
        out_shape=pltpu.VMEM((rows, width), BF16),
        in_specs=[anywhere] * 7,
        out_specs=pl.BlockSpec(memory_space=pltpu.VMEM),
        scratch_shapes=[
            pltpu.VMEM((pairs, rows, 2 * feats), BF16),
            pltpu.VMEM((total, width), BF16),
            pltpu.VMEM((total, width), BF16),
            pltpu.VMEM((total, width), BF16),
            pltpu.VMEM((rows, width), F32),
            pltpu.VMEM((rows, width), F32),
            pltpu.VMEM((rows, width), F32),
            pltpu.VMEM((rows, width), F32),
            pltpu.VMEM((heads, rows, max(depth, 1) * hd), BF16),
            pltpu.VMEM((depth + 1, rows, width), F32),
            pltpu.VMEM((heads, hd, hd), F32),
            pltpu.VMEM((heads, max(depth, 1) * hd, hd), BF16),
            pltpu.VMEM((heads, hd, hd), BF16),
            pltpu.VMEM((rows, width), BF16),
            pltpu.VMEM((rows, width), BF16),
            pltpu.VMEM((len(GROUPS), heads, hd, hd), BF16),
            pltpu.VMEM((sum(row_chunks(rows)[n][1] for n in AIDED), feats), BF16),
            pltpu.VMEM(level_index.shape, jnp.int32),
            pltpu.VMEM((1, width), F32),
            pltpu.SMEM((heads, quant), F32),
            pltpu.VMEM((quant, width), F32),
            pltpu.VMEM((3 * quant, width), BF16),
            dma((7,)),
            dma((n_chunk,)),
            dma((far, n_chunk)),
            dma((far, n_chunk)),
            dma((pairs, 2, n_chunk)),
            dma((heads, CUTS)),
            dma((heads, max(depth, 1), CUTS)),
            dma((heads, max(depth, 1), CUTS)),
            dma((len(AIDED),)),
            dma((len(AIDED),)),
            dma((len(AIDED),)),
        ],
        compiler_params=pltpu.CompilerParams(
            collective_id=0, has_side_effects=True, vmem_limit_bytes=56 * 1024 * 1024
        ),
    )(tokens, q_weight, k_weight, v_weight, level_table, level_index, out_gain.reshape(1, width))
    return result


def solution(mesh):
    return jax.shard_map(
        functools.partial(on_device, mesh.shape["head"], mesh.shape["seq"]),
        mesh=mesh,
        in_specs=(
            P(("groups", "seq"), "head"),
            P(None, "head"),
            P(None, "head"),
            P(None, "head"),
            P("head", None),
            P(None, ("groups", "seq")),
            P("head"),
        ),
        out_specs=P(("groups", "seq"), "head"),
        check_vma=False,
    )
```

```python
import functools

import jax
import jax.numpy as jnp
from jax import lax
from jax.experimental import pallas as pl
from jax.experimental.pallas import tpu as pltpu
from jax.sharding import PartitionSpec as P

MESH = pl.DeviceIdType.MESH
F32 = jnp.float32
BF16 = jnp.bfloat16
EPS = 1e-06
SHARES = (16, 16, 9, 3, 4, 8, 6, 2)
CHUNKS = (1, 1, 3, 1, 2)
AIDED = (2, 3)
GROUPS = (1, 1, 1, 1, 1)
DUAL = 1
CUTS = 2


def row_chunks(rows):
    sizes = [rows // sum(SHARES) * part for part in SHARES]
    starts, at = [], 0
    for size in sizes:
        starts.append((at, size))
        at += size
    return starts


def fused(
    n_head, n_seq, depth,
    tok, wq_in, wk_in, wv_in, table_in, index_in, gain_in,
    out,
    gat, wq, wk, wv, acc_q, acc_k, acc_v, local, scaled_q, lev, state, merged, outbox,
    keys, vals, prior, guests,
    index, gain, table, wide, parts,
    load_sem, near_send, far_send, relay_send, recv_sem, up_send, pass_send, up_recv, aid_send, aid_recv, back_send,
):
    rows, feats = tok.shape
    width = wq_in.shape[1]
    heads, quant = table.shape
    hd = width // heads
    part_rows = hd // CUTS
    pieces = row_chunks(rows)
    relayed = len(pieces) - DUAL
    parts_of, spans, chunks, firsts = [], [], [], []
    for n in CHUNKS:
        first = sum(map(len, parts_of))
        parts_of.append(list(range(first, first + n)))
        chunks.append((pieces[first][0], sum(size for _, size in pieces[first:first + n])))
    for n in GROUPS:
        first = sum(GROUPS[:len(firsts)])
        firsts.append(first)
        spans.append((chunks[first][0], sum(chunks[first + n - 1])))
    me = lax.axis_index("head")
    block = lax.axis_index("seq")
    pair = me // 2
    side = me % 2
    partner = pair * 2 + 1 - side
    n_pair = n_head // 2
    far_pairs = [(pair + 1 + j) % n_pair for j in range(n_pair - 1)]
    aided = AIDED if n_pair == 2 and n_seq > 1 else ()

    def is_aided(n, b):
        if n == AIDED[0]:
            return (b >= 0) & (b < n_seq - 1)
        return b == n_seq - 2

    def cols_of(s):
        return pl.ds(pl.multiple_of(s * feats, feats), feats)

    def wrows(p):
        return pl.ds(pl.multiple_of(p * (2 * feats), 2 * feats), 2 * feats)

    def wpart(p, s):
        return pl.ds(pl.multiple_of((p * 2 + s) * feats, feats), feats)

    loads = [
        pltpu.make_async_copy(tok, gat.at[pair, :, cols_of(side)], load_sem.at[0]),
        pltpu.make_async_copy(wk_in, wk, load_sem.at[1]),
        pltpu.make_async_copy(wv_in, wv, load_sem.at[2]),
        pltpu.make_async_copy(wq_in, wq, load_sem.at[3]),
        pltpu.make_async_copy(index_in, index, load_sem.at[4]),
        pltpu.make_async_copy(gain_in, gain, load_sem.at[5]),
        pltpu.make_async_copy(table_in, table, load_sem.at[6]),
    ]
    barrier = pltpu.get_barrier_semaphore()
    for p in far_pairs:
        for s in (side, 1 - side)[:1 + min(DUAL, 1)]:
            pl.semaphore_signal(barrier, inc=1, device_id={"head": p * 2 + s}, device_id_type=MESH)
    pl.semaphore_signal(barrier, inc=1, device_id={"head": partner}, device_id_type=MESH)

    @pl.when(block > 0)
    def _():
        pl.semaphore_signal(barrier, inc=1, device_id={"seq": block - 1}, device_id_type=MESH)

    @pl.when(block < n_seq - 1)
    def _():
        pl.semaphore_signal(barrier, inc=1, device_id={"seq": block + 1}, device_id_type=MESH)

    if aided:
        for b in (block - 1, block + 1):
            @pl.when((b >= 0) & (b < n_seq))
            def _():
                pl.semaphore_signal(
                    barrier, inc=1, device_id={"head": far_pairs[0] * 2 + side, "seq": b}, device_id_type=MESH
                )

    for n in (6, 4, 5, 0, 1, 2, 3):
        loads[n].start()

    beside = (block + n_seq - 1) // n_seq + (2 * n_seq - 2 - block) // n_seq
    pl.semaphore_wait(barrier, 1 + (n_pair - 1) * (1 + min(DUAL, 1)) + beside * (2 if aided else 1))

    def piece(p, s, c):
        at, size = pieces[c]
        return gat.at[p, pl.ds(at, size), cols_of(s)]

    def far_copy(j, c):
        at, size = pieces[c]
        return pltpu.make_async_remote_copy(
            src_ref=tok.at[pl.ds(at, size), :], dst_ref=piece(pair, side, c),
            send_sem=far_send.at[j, c], recv_sem=recv_sem.at[pair, side, c],
            device_id={"head": far_pairs[j] * 2 + side}, device_id_type=MESH,
        )

    def cross_copy(j, c):
        at, size = pieces[c]
        return pltpu.make_async_remote_copy(
            src_ref=tok.at[pl.ds(at, size), :], dst_ref=piece(pair, side, c),
            send_sem=relay_send.at[j, c], recv_sem=recv_sem.at[pair, side, c],
            device_id={"head": far_pairs[j] * 2 + 1 - side}, device_id_type=MESH,
        )

    def spot(n):
        at = sum(pieces[a][1] for a in AIDED[:AIDED.index(n)])
        return guests.at[pl.ds(at, pieces[n][1]), :]

    def aid_copy(n):
        at, size = pieces[n]
        return pltpu.make_async_remote_copy(
            src_ref=tok.at[pl.ds(at, size), :], dst_ref=spot(n),
            send_sem=aid_send.at[AIDED.index(n)], recv_sem=aid_recv.at[AIDED.index(n)],
            device_id={"head": far_pairs[0] * 2 + side, "seq": block + 1}, device_id_type=MESH,
        )

    def back_copy(n):
        return pltpu.make_async_remote_copy(
            src_ref=spot(n), dst_ref=piece(far_pairs[0], side, n),
            send_sem=back_send.at[AIDED.index(n)], recv_sem=recv_sem.at[far_pairs[0], side, n],
            device_id={"seq": block - 1}, device_id_type=MESH,
        )

    def near_copy(c):
        at, size = pieces[c]
        return pltpu.make_async_remote_copy(
            src_ref=tok.at[pl.ds(at, size), :], dst_ref=piece(pair, side, c),
            send_sem=near_send.at[c], recv_sem=recv_sem.at[pair, side, c],
            device_id={"head": partner}, device_id_type=MESH,
        )

    def relay_copy(j, c):
        p = far_pairs[j]
        return pltpu.make_async_remote_copy(
            src_ref=piece(p, side, c), dst_ref=piece(p, side, c),
            send_sem=relay_send.at[j, c], recv_sem=recv_sem.at[p, side, c],
            device_id={"head": partner}, device_id_type=MESH,
        )

    def arrived(p, s, c):
        here = piece(p, s, c)
        pltpu.make_async_remote_copy(
            src_ref=here, dst_ref=here, send_sem=near_send.at[c], recv_sem=recv_sem.at[p, s, c],
            device_id={"head": partner}, device_id_type=MESH,
        ).wait_recv()

    for n in aided:
        @pl.when(is_aided(n, block))
        def _():
            aid_copy(n).start()
    for c in range(len(pieces)):
        for j in range(n_pair - 1):
            if c in aided:
                @pl.when(jnp.logical_not(is_aided(c, block)))
                def _():
                    far_copy(j, c).start()
            else:
                far_copy(j, c).start()
            if c >= relayed:
                cross_copy(j, c).start()
        near_copy(c).start()

    for level in range(depth):
        @pl.when(block // 2**level % 2 == 0)
        def _():
            merged[:, level * hd:(level + 1) * hd, :] = jnp.zeros((heads, hd, hd), BF16)
    state[...] = jnp.zeros_like(state)

    loads[6].wait()
    for q in range(quant):
        for h in range(heads):
            wide[q:q + 1, h * hd:(h + 1) * hd] = jnp.full((1, hd), table[h, q], F32)
    top = wide[...].astype(BF16)
    rest = wide[...] - top.astype(F32)
    mid = rest.astype(BF16)
    low = (rest - mid.astype(F32)).astype(BF16)
    parts[...] = jnp.concatenate([top, mid, low], axis=0)
    loads[4].wait()
    loads[5].wait()

    step = min(rows, 256)
    for level in range(depth + 1):
        for at in range(0, rows, step):
            column = jnp.broadcast_to(index[level:level + 1, at:at + step], (3 * quant, step))
            ids = lax.broadcasted_iota(jnp.int32, (3 * quant, step), 0) % quant
            one_hot = jnp.where(column == ids, 1.0, 0.0).astype(BF16)
            lev[level, at:at + step, :] = lax.dot_general(
                one_hot, parts[...], (((0,), (0,)), ((), ())), preferred_element_type=F32
            )

    loads[0].wait()
    for copy in loads[1:4]:
        copy.wait()
    for c in range(len(pieces)):
        arrived(pair, 1 - side, c)
    for at in range(0, rows, step):
        here = gat[pair, at:at + step, :]
        for acc, w in ((acc_k, wk), (acc_v, wv), (acc_q, wq)):
            acc[at:at + step, :] = jnp.dot(here, w[wrows(pair), :], preferred_element_type=F32)

    def state_part(level, u):
        return pl.ds(level * hd + u * part_rows, part_rows)

    def up_copy(h, u, level):
        return pltpu.make_async_remote_copy(
            src_ref=outbox.at[h, pl.ds(u * part_rows, part_rows), :],
            dst_ref=merged.at[h, state_part(level, u), :],
            send_sem=up_send.at[h, u], recv_sem=up_recv.at[h, level, u],
            device_id={"seq": block + 1}, device_id_type=MESH,
        )

    def pass_copy(h, u, level):
        here = merged.at[h, state_part(level, u), :]
        return pltpu.make_async_remote_copy(
            src_ref=here, dst_ref=here,
            send_sem=pass_send.at[h, level, u], recv_sem=up_recv.at[h, level, u],
            device_id={"seq": block + 1}, device_id_type=MESH,
        )

    def add_far(total, here, w, p):
        return total + jnp.dot(here, w[wrows(p), :], preferred_element_type=F32)

    def take(c):
        for n in parts_of[c]:
            if n < relayed:
                for j, p in enumerate(far_pairs):
                    arrived(p, side, n)
                    relay_copy(j, n).start()

    def add_side(totals, c, s):
        at, size = chunks[c]
        for p in far_pairs:
            here = gat[p, at:at + size, cols_of(s)]
            totals = [
                total + jnp.dot(here, w[wpart(p, s), :], preferred_element_type=F32)
                for total, w in zip(totals, (wk, wv))
            ]
        return totals

    def keys_and_values(c):
        at, size = chunks[c]
        last = c == len(chunks) - 1
        totals = [acc_k[at:at + size, :], acc_v[at:at + size, :]]
        for n in parts_of[c]:
            if n >= relayed:
                for p in far_pairs:
                    arrived(p, side, n)
        if last:
            totals = add_side(totals, c, side)
        for n in parts_of[c]:
            for p in far_pairs:
                arrived(p, 1 - side, n)
        if last:
            totals = add_side(totals, c, 1 - side)
        else:
            for p in far_pairs:
                here = gat[p, at:at + size, :]
                totals = [add_far(total, here, w, p) for total, w in zip(totals, (wk, wv))]
        raw_k, raw_v = totals
        k_of, v_of = [], []
        for h in range(heads):
            cut = slice(h * hd, (h + 1) * hd)
            k = raw_k[:, cut]
            k_of.append((k * lax.rsqrt(jnp.sum(k * k, -1, keepdims=True) + EPS)).astype(BF16))
            v_of.append(raw_v[:, cut].astype(BF16))
        grown = [
            lax.dot_general(k, v, (((0,), (0,)), ((), ())), preferred_element_type=F32)
            for k, v in zip(k_of, v_of)
        ]
        for h in range(heads):
            cut = slice(h * hd, (h + 1) * hd)
            before = state[h]
            if c in firsts:
                prior[firsts.index(c), h] = before.astype(BF16)
            after = before + grown[h]
            state[h] = after
            if last:
                outbox[h] = after.astype(BF16)
        if last and depth > 0:
            @pl.when(block % 2 == 0)
            def _():
                for h in range(heads):
                    for u in range(CUTS):
                        up_copy(h, u, 0).start()
        for h in range(heads):
            cut = slice(h * hd, (h + 1) * hd)
            keys[at:at + size, cut] = k_of[h]
            vals[at:at + size, cut] = v_of[h]

    def queries(g):
        at, end = spans[g]
        size = end - at
        raw_q = acc_q[at:end, :]
        for p in far_pairs:
            raw_q = add_far(raw_q, gat[p, at:end, :], wq, p)
        cuts = [slice(h * hd, (h + 1) * hd) for h in range(heads)]
        own_of = []
        for h, cut in enumerate(cuts):
            q = raw_q[:, cut]
            q = q * lax.rsqrt(jnp.sum(q * q, -1, keepdims=True) + EPS)
            own_of.append((q * lev[0, at:end, cut]).astype(BF16))
            for level in range(depth):
                scaled_q[h, at:end, level * hd:(level + 1) * hd] = (
                    q * lev[level + 1, at:end, cut]
                ).astype(BF16)
        causal = lax.broadcasted_iota(jnp.int32, (size, size), 0) >= lax.broadcasted_iota(
            jnp.int32, (size, size), 1
        )
        scores_of = [
            lax.dot_general(
                own_of[h], keys[at:end, cut], (((1,), (1,)), ((), ())), preferred_element_type=F32
            )
            for h, cut in enumerate(cuts)
        ]
        scores_of = [jnp.where(causal, scores, 0.0).astype(BF16) for scores in scores_of]
        for h, cut in enumerate(cuts):
            local[at:end, cut] = jnp.dot(
                scores_of[h], vals[at:end, cut], preferred_element_type=F32
            ) + jnp.dot(own_of[h], prior[g, h], preferred_element_type=F32)

    for n in aided:
        @pl.when(is_aided(n, block - 1))
        def _():
            aid_copy(n).wait_recv()
            back_copy(n).start()
    take(0)
    for c in range(len(chunks)):
        if c + 1 < len(chunks):
            take(c + 1)
        keys_and_values(c)
        if c + 1 in firsts:
            queries(firsts.index(c + 1) - 1)

    def wait_level(h, level):
        @pl.when(block // 2**level % 2 == 1)
        def _():
            for u in range(CUTS):
                pass_copy(h, u, level).wait_recv()

    def forward(h):
        for level in range(depth):
            for u in range(CUTS):
                @pl.when(block // 2**level % 2 == 1)
                def _():
                    pass_copy(h, u, level).wait_recv()
                if level > 0:
                    @pl.when((block // 2**level % 2 == 1) & (block % 2**level != 2**level - 1))
                    def _():
                        pass_copy(h, u, level).start()

                    @pl.when(block % 2 ** (level + 1) == 2**level - 1)
                    def _():
                        mine = pl.ds(u * part_rows, part_rows)
                        total = state[h, mine, :]
                        for below in range(level):
                            total = total + merged[h, state_part(below, u), :].astype(F32)
                        outbox[h, mine, :] = total.astype(BF16)
                        up_copy(h, u, level).start()

    def last_queries():
        queries(len(spans) - 1)

    def finish(h):
        cut = slice(h * hd, (h + 1) * hd)
        tile = min(rows, 256)
        for at in range(0, rows, tile):
            both = local[at:at + tile, cut]
            if depth > 0:
                both = both + jnp.dot(
                    scaled_q[h, at:at + tile, :], merged[h], preferred_element_type=F32
                )
            scale = lax.rsqrt(jnp.sum(both * both, -1, keepdims=True) * (1.0 / hd) + EPS)
            out[at:at + tile, cut] = (both * scale * gain[:, cut]).astype(BF16)

    if depth > 0:
        @pl.when((block % 2 == 1) & (block < n_seq - 1))
        def _():
            for h in range(heads):
                forward(h)

    last_queries()

    if depth > 0:
        @pl.when((block % 2 == 0) & (block < n_seq - 1))
        def _():
            for h in range(heads):
                forward(h)

    @pl.when(block < n_seq - 1)
    def _():
        for h in range(heads):
            finish(h)

    @pl.when(block == n_seq - 1)
    def _():
        for h in range(heads):
            for level in range(depth):
                wait_level(h, level)
            finish(h)

    for n in aided:
        @pl.when(is_aided(n, block))
        def _():
            aid_copy(n).wait_send()

        @pl.when(is_aided(n, block - 1))
        def _():
            back_copy(n).wait_send()
    for c in range(len(pieces)):
        near_copy(c).wait_send()
        for j in range(n_pair - 1):
            if c in aided:
                @pl.when(jnp.logical_not(is_aided(c, block)))
                def _():
                    far_copy(j, c).wait_send()
            else:
                far_copy(j, c).wait_send()
            (relay_copy if c < relayed else cross_copy)(j, c).wait_send()
    for h in range(heads):
        for u in range(CUTS):
            if depth > 0:
                @pl.when(block < n_seq - 1)
                def _():
                    up_copy(h, u, 0).wait_send()
            for level in range(1, depth):
                @pl.when((block // 2**level % 2 == 1) & (block % 2**level != 2**level - 1))
                def _():
                    pass_copy(h, u, level).wait_send()


def on_device(n_head, n_seq, tokens, q_weight, k_weight, v_weight, level_table, level_index, out_gain):
    rows, feats = tokens.shape
    total, width = q_weight.shape
    heads, quant = level_table.shape
    hd = width // heads
    depth = min(n_seq.bit_length() - 1, level_index.shape[0] - 1)
    pairs = n_head // 2
    far = max(pairs - 1, 1)
    n_chunk = len(SHARES)
    dma = pltpu.SemaphoreType.DMA
    anywhere = pl.BlockSpec(memory_space=pltpu.HBM)
    result = pl.pallas_call(
        functools.partial(fused, n_head, n_seq, depth),
        out_shape=pltpu.VMEM((rows, width), BF16),
        in_specs=[anywhere] * 7,
        out_specs=pl.BlockSpec(memory_space=pltpu.VMEM),
        scratch_shapes=[
            pltpu.VMEM((pairs, rows, 2 * feats), BF16),
            pltpu.VMEM((total, width), BF16),
            pltpu.VMEM((total, width), BF16),
            pltpu.VMEM((total, width), BF16),
            pltpu.VMEM((rows, width), F32),
            pltpu.VMEM((rows, width), F32),
            pltpu.VMEM((rows, width), F32),
            pltpu.VMEM((rows, width), F32),
            pltpu.VMEM((heads, rows, max(depth, 1) * hd), BF16),
            pltpu.VMEM((depth + 1, rows, width), F32),
            pltpu.VMEM((heads, hd, hd), F32),
            pltpu.VMEM((heads, max(depth, 1) * hd, hd), BF16),
            pltpu.VMEM((heads, hd, hd), BF16),
            pltpu.VMEM((rows, width), BF16),
            pltpu.VMEM((rows, width), BF16),
            pltpu.VMEM((len(GROUPS), heads, hd, hd), BF16),
            pltpu.VMEM((sum(row_chunks(rows)[n][1] for n in AIDED), feats), BF16),
            pltpu.VMEM(level_index.shape, jnp.int32),
            pltpu.VMEM((1, width), F32),
            pltpu.SMEM((heads, quant), F32),
            pltpu.VMEM((quant, width), F32),
            pltpu.VMEM((3 * quant, width), BF16),
            dma((7,)),
            dma((n_chunk,)),
            dma((far, n_chunk)),
            dma((far, n_chunk)),
            dma((pairs, 2, n_chunk)),
            dma((heads, CUTS)),
            dma((heads, max(depth, 1), CUTS)),
            dma((heads, max(depth, 1), CUTS)),
            dma((len(AIDED),)),
            dma((len(AIDED),)),
            dma((len(AIDED),)),
        ],
        compiler_params=pltpu.CompilerParams(
            collective_id=0, has_side_effects=True, vmem_limit_bytes=56 * 1024 * 1024
        ),
    )(tokens, q_weight, k_weight, v_weight, level_table, level_index, out_gain.reshape(1, width))
    return result


def solution(mesh):
    return jax.shard_map(
        functools.partial(on_device, mesh.shape["head"], mesh.shape["seq"]),
        mesh=mesh,
        in_specs=(
            P(("groups", "seq"), "head"),
            P(None, "head"),
            P(None, "head"),
            P(None, "head"),
            P("head", None),
            P(None, ("groups", "seq")),
            P("head"),
        ),
        out_specs=P(("groups", "seq"), "head"),
        check_vma=False,
    )
```

```python
import functools

import jax
import jax.numpy as jnp
from jax import lax
from jax.experimental import pallas as pl
from jax.experimental.pallas import tpu as pltpu
from jax.sharding import PartitionSpec as P

MESH = pl.DeviceIdType.MESH
F32 = jnp.float32
BF16 = jnp.bfloat16
EPS = 1e-06
SHARES = (16, 16, 9, 3, 4, 8, 6, 2)
CHUNKS = (1, 1, 3, 1, 2)
AIDED = (2, 3)
GROUPS = (1, 1, 1, 1, 1)
DUAL = 1
CUTS = 1


def row_chunks(rows):
    sizes = [rows // sum(SHARES) * part for part in SHARES]
    starts, at = [], 0
    for size in sizes:
        starts.append((at, size))
        at += size
    return starts


def fused(
    n_head, n_seq, depth,
    tok, wq_in, wk_in, wv_in, table_in, index_in, gain_in,
    out,
    gat, wq, wk, wv, acc_q, acc_k, acc_v, local, scaled_q, lev, state, merged, outbox,
    keys, vals, prior, guests,
    index, gain, table, wide, parts,
    load_sem, near_send, far_send, relay_send, recv_sem, up_send, pass_send, up_recv, aid_send, aid_recv, back_send,
):
    rows, feats = tok.shape
    width = wq_in.shape[1]
    heads, quant = table.shape
    hd = width // heads
    part_rows = hd // CUTS
    pieces = row_chunks(rows)
    relayed = len(pieces) - DUAL
    parts_of, spans, chunks, firsts = [], [], [], []
    for n in CHUNKS:
        first = sum(map(len, parts_of))
        parts_of.append(list(range(first, first + n)))
        chunks.append((pieces[first][0], sum(size for _, size in pieces[first:first + n])))
    for n in GROUPS:
        first = sum(GROUPS[:len(firsts)])
        firsts.append(first)
        spans.append((chunks[first][0], sum(chunks[first + n - 1])))
    me = lax.axis_index("head")
    block = lax.axis_index("seq")
    pair = me // 2
    side = me % 2
    partner = pair * 2 + 1 - side
    n_pair = n_head // 2
    far_pairs = [(pair + 1 + j) % n_pair for j in range(n_pair - 1)]
    aided = AIDED if n_pair == 2 and n_seq > 1 else ()

    def is_aided(n, b):
        if n == AIDED[0]:
            return (b >= 0) & (b < n_seq - 1)
        return b == n_seq - 2

    def cols_of(s):
        return pl.ds(pl.multiple_of(s * feats, feats), feats)

    def wrows(p):
        return pl.ds(pl.multiple_of(p * (2 * feats), 2 * feats), 2 * feats)

    def wpart(p, s):
        return pl.ds(pl.multiple_of((p * 2 + s) * feats, feats), feats)

    loads = [
        pltpu.make_async_copy(tok, gat.at[pair, :, cols_of(side)], load_sem.at[0]),
        pltpu.make_async_copy(wk_in, wk, load_sem.at[1]),
        pltpu.make_async_copy(wv_in, wv, load_sem.at[2]),
        pltpu.make_async_copy(wq_in, wq, load_sem.at[3]),
        pltpu.make_async_copy(index_in, index, load_sem.at[4]),
        pltpu.make_async_copy(gain_in, gain, load_sem.at[5]),
        pltpu.make_async_copy(table_in, table, load_sem.at[6]),
    ]
    barrier = pltpu.get_barrier_semaphore()
    for p in far_pairs:
        for s in (side, 1 - side)[:1 + min(DUAL, 1)]:
            pl.semaphore_signal(barrier, inc=1, device_id={"head": p * 2 + s}, device_id_type=MESH)
    pl.semaphore_signal(barrier, inc=1, device_id={"head": partner}, device_id_type=MESH)

    @pl.when(block > 0)
    def _():
        pl.semaphore_signal(barrier, inc=1, device_id={"seq": block - 1}, device_id_type=MESH)

    @pl.when(block < n_seq - 1)
    def _():
        pl.semaphore_signal(barrier, inc=1, device_id={"seq": block + 1}, device_id_type=MESH)

    if aided:
        for b in (block - 1, block + 1):
            @pl.when((b >= 0) & (b < n_seq))
            def _():
                pl.semaphore_signal(
                    barrier, inc=1, device_id={"head": far_pairs[0] * 2 + side, "seq": b}, device_id_type=MESH
                )

    for n in (6, 4, 5, 0, 1, 2, 3):
        loads[n].start()

    beside = (block + n_seq - 1) // n_seq + (2 * n_seq - 2 - block) // n_seq
    pl.semaphore_wait(barrier, 1 + (n_pair - 1) * (1 + min(DUAL, 1)) + beside * (2 if aided else 1))

    def piece(p, s, c):
        at, size = pieces[c]
        return gat.at[p, pl.ds(at, size), cols_of(s)]

    def far_copy(j, c):
        at, size = pieces[c]
        return pltpu.make_async_remote_copy(
            src_ref=tok.at[pl.ds(at, size), :], dst_ref=piece(pair, side, c),
            send_sem=far_send.at[j, c], recv_sem=recv_sem.at[pair, side, c],
            device_id={"head": far_pairs[j] * 2 + side}, device_id_type=MESH,
        )

    def cross_copy(j, c):
        at, size = pieces[c]
        return pltpu.make_async_remote_copy(
            src_ref=tok.at[pl.ds(at, size), :], dst_ref=piece(pair, side, c),
            send_sem=relay_send.at[j, c], recv_sem=recv_sem.at[pair, side, c],
            device_id={"head": far_pairs[j] * 2 + 1 - side}, device_id_type=MESH,
        )

    def spot(n):
        at = sum(pieces[a][1] for a in AIDED[:AIDED.index(n)])
        return guests.at[pl.ds(at, pieces[n][1]), :]

    def aid_copy(n):
        at, size = pieces[n]
        return pltpu.make_async_remote_copy(
            src_ref=tok.at[pl.ds(at, size), :], dst_ref=spot(n),
            send_sem=aid_send.at[AIDED.index(n)], recv_sem=aid_recv.at[AIDED.index(n)],
            device_id={"head": far_pairs[0] * 2 + side, "seq": block + 1}, device_id_type=MESH,
        )

    def back_copy(n):
        return pltpu.make_async_remote_copy(
            src_ref=spot(n), dst_ref=piece(far_pairs[0], side, n),
            send_sem=back_send.at[AIDED.index(n)], recv_sem=recv_sem.at[far_pairs[0], side, n],
            device_id={"seq": block - 1}, device_id_type=MESH,
        )

    near_copy = pltpu.make_async_remote_copy(
        src_ref=tok, dst_ref=gat.at[pair, :, cols_of(side)],
        send_sem=near_send.at[0], recv_sem=near_send.at[1],
        device_id={"head": partner}, device_id_type=MESH,
    )

    def relay_copy(j, c):
        p = far_pairs[j]
        return pltpu.make_async_remote_copy(
            src_ref=piece(p, side, c), dst_ref=piece(p, side, c),
            send_sem=relay_send.at[j, c], recv_sem=recv_sem.at[p, side, c],
            device_id={"head": partner}, device_id_type=MESH,
        )

    def arrived(p, s, c):
        here = piece(p, s, c)
        pltpu.make_async_remote_copy(
            src_ref=here, dst_ref=here, send_sem=near_send.at[0], recv_sem=recv_sem.at[p, s, c],
            device_id={"head": partner}, device_id_type=MESH,
        ).wait_recv()

    for n in aided:
        @pl.when(is_aided(n, block))
        def _():
            aid_copy(n).start()
    for c in range(len(pieces)):
        for j in range(n_pair - 1):
            if c in aided:
                @pl.when(jnp.logical_not(is_aided(c, block)))
                def _():
                    far_copy(j, c).start()
            else:
                far_copy(j, c).start()
            if c >= relayed:
                cross_copy(j, c).start()
        if c == 0:
            near_copy.start()

    for level in range(depth):
        @pl.when(block // 2**level % 2 == 0)
        def _():
            merged[:, level * hd:(level + 1) * hd, :] = jnp.zeros((heads, hd, hd), BF16)
    state[...] = jnp.zeros_like(state)

    loads[6].wait()
    for q in range(quant):
        for h in range(heads):
            wide[q:q + 1, h * hd:(h + 1) * hd] = jnp.full((1, hd), table[h, q], F32)
    top = wide[...].astype(BF16)
    rest = wide[...] - top.astype(F32)
    mid = rest.astype(BF16)
    low = (rest - mid.astype(F32)).astype(BF16)
    parts[...] = jnp.concatenate([top, mid, low], axis=0)
    loads[4].wait()
    loads[5].wait()

    step = min(rows, 256)
    for level in range(depth + 1):
        for at in range(0, rows, step):
            column = jnp.broadcast_to(index[level:level + 1, at:at + step], (3 * quant, step))
            ids = lax.broadcasted_iota(jnp.int32, (3 * quant, step), 0) % quant
            one_hot = jnp.where(column == ids, 1.0, 0.0).astype(BF16)
            lev[level, at:at + step, :] = lax.dot_general(
                one_hot, parts[...], (((0,), (0,)), ((), ())), preferred_element_type=F32
            )

    loads[0].wait()
    for copy in loads[1:4]:
        copy.wait()
    near_copy.wait_recv()
    for at in range(0, rows, step):
        here = gat[pair, at:at + step, :]
        for acc, w in ((acc_k, wk), (acc_v, wv), (acc_q, wq)):
            acc[at:at + step, :] = jnp.dot(here, w[wrows(pair), :], preferred_element_type=F32)

    def state_part(level, u):
        return pl.ds(level * hd + u * part_rows, part_rows)

    def up_copy(h, u, level):
        return pltpu.make_async_remote_copy(
            src_ref=outbox.at[h, pl.ds(u * part_rows, part_rows), :],
            dst_ref=merged.at[h, state_part(level, u), :],
            send_sem=up_send.at[h, u], recv_sem=up_recv.at[h, level, u],
            device_id={"seq": block + 1}, device_id_type=MESH,
        )

    def pass_copy(h, u, level):
        here = merged.at[h, state_part(level, u), :]
        return pltpu.make_async_remote_copy(
            src_ref=here, dst_ref=here,
            send_sem=pass_send.at[h, level, u], recv_sem=up_recv.at[h, level, u],
            device_id={"seq": block + 1}, device_id_type=MESH,
        )

    def add_far(total, here, w, p):
        return total + jnp.dot(here, w[wrows(p), :], preferred_element_type=F32)

    def take(c):
        for n in parts_of[c]:
            if n < relayed:
                for j, p in enumerate(far_pairs):
                    arrived(p, side, n)
                    relay_copy(j, n).start()

    def add_side(totals, c, s):
        at, size = chunks[c]
        for p in far_pairs:
            here = gat[p, at:at + size, cols_of(s)]
            totals = [
                total + jnp.dot(here, w[wpart(p, s), :], preferred_element_type=F32)
                for total, w in zip(totals, (wk, wv))
            ]
        return totals

    def keys_and_values(c):
        at, size = chunks[c]
        last = c == len(chunks) - 1
        totals = [acc_k[at:at + size, :], acc_v[at:at + size, :]]
        for n in parts_of[c]:
            if n >= relayed:
                for p in far_pairs:
                    arrived(p, side, n)
        if last:
            totals = add_side(totals, c, side)
        for n in parts_of[c]:
            for p in far_pairs:
                arrived(p, 1 - side, n)
        if last:
            totals = add_side(totals, c, 1 - side)
        else:
            for p in far_pairs:
                here = gat[p, at:at + size, :]
                totals = [add_far(total, here, w, p) for total, w in zip(totals, (wk, wv))]
        raw_k, raw_v = totals
        k_of, v_of = [], []
        for h in range(heads):
            cut = slice(h * hd, (h + 1) * hd)
            k = raw_k[:, cut]
            k_of.append((k * lax.rsqrt(jnp.sum(k * k, -1, keepdims=True) + EPS)).astype(BF16))
            v_of.append(raw_v[:, cut].astype(BF16))
        grown = [
            lax.dot_general(k, v, (((0,), (0,)), ((), ())), preferred_element_type=F32)
            for k, v in zip(k_of, v_of)
        ]
        for h in range(heads):
            cut = slice(h * hd, (h + 1) * hd)
            before = state[h]
            if c in firsts:
                prior[firsts.index(c), h] = before.astype(BF16)
            after = before + grown[h]
            state[h] = after
            if last:
                outbox[h] = after.astype(BF16)
        if last and depth > 0:
            @pl.when(block % 2 == 0)
            def _():
                for h in range(heads):
                    for u in range(CUTS):
                        up_copy(h, u, 0).start()
        for h in range(heads):
            cut = slice(h * hd, (h + 1) * hd)
            keys[at:at + size, cut] = k_of[h]
            vals[at:at + size, cut] = v_of[h]

    def queries(g):
        at, end = spans[g]
        size = end - at
        raw_q = acc_q[at:end, :]
        for p in far_pairs:
            raw_q = add_far(raw_q, gat[p, at:end, :], wq, p)
        cuts = [slice(h * hd, (h + 1) * hd) for h in range(heads)]
        own_of = []
        for h, cut in enumerate(cuts):
            q = raw_q[:, cut]
            q = q * lax.rsqrt(jnp.sum(q * q, -1, keepdims=True) + EPS)
            own_of.append((q * lev[0, at:end, cut]).astype(BF16))
            for level in range(depth):
                scaled_q[h, at:end, level * hd:(level + 1) * hd] = (
                    q * lev[level + 1, at:end, cut]
                ).astype(BF16)
        causal = lax.broadcasted_iota(jnp.int32, (size, size), 0) >= lax.broadcasted_iota(
            jnp.int32, (size, size), 1
        )
        scores_of = [
            lax.dot_general(
                own_of[h], keys[at:end, cut], (((1,), (1,)), ((), ())), preferred_element_type=F32
            )
            for h, cut in enumerate(cuts)
        ]
        scores_of = [jnp.where(causal, scores, 0.0).astype(BF16) for scores in scores_of]
        for h, cut in enumerate(cuts):
            local[at:end, cut] = jnp.dot(
                scores_of[h], vals[at:end, cut], preferred_element_type=F32
            ) + jnp.dot(own_of[h], prior[g, h], preferred_element_type=F32)

    for n in aided:
        @pl.when(is_aided(n, block - 1))
        def _():
            aid_copy(n).wait_recv()
            back_copy(n).start()
    take(0)
    for c in range(len(chunks)):
        if c + 1 < len(chunks):
            take(c + 1)
        keys_and_values(c)
        if c + 1 in firsts:
            queries(firsts.index(c + 1) - 1)

    def wait_level(h, level):
        @pl.when(block // 2**level % 2 == 1)
        def _():
            for u in range(CUTS):
                pass_copy(h, u, level).wait_recv()

    def forward(h):
        for level in range(depth):
            for u in range(CUTS):
                @pl.when(block // 2**level % 2 == 1)
                def _():
                    pass_copy(h, u, level).wait_recv()
                if level > 0:
                    @pl.when((block // 2**level % 2 == 1) & (block % 2**level != 2**level - 1))
                    def _():
                        pass_copy(h, u, level).start()

                    @pl.when(block % 2 ** (level + 1) == 2**level - 1)
                    def _():
                        mine = pl.ds(u * part_rows, part_rows)
                        total = state[h, mine, :]
                        for below in range(level):
                            total = total + merged[h, state_part(below, u), :].astype(F32)
                        outbox[h, mine, :] = total.astype(BF16)
                        up_copy(h, u, level).start()

    def last_queries():
        queries(len(spans) - 1)

    def finish(h):
        cut = slice(h * hd, (h + 1) * hd)
        tile = min(rows, 256)
        for at in range(0, rows, tile):
            both = local[at:at + tile, cut]
            if depth > 0:
                both = both + jnp.dot(
                    scaled_q[h, at:at + tile, :], merged[h], preferred_element_type=F32
                )
            scale = lax.rsqrt(jnp.sum(both * both, -1, keepdims=True) * (1.0 / hd) + EPS)
            out[at:at + tile, cut] = (both * scale * gain[:, cut]).astype(BF16)

    if depth > 0:
        @pl.when((block % 2 == 1) & (block < n_seq - 1))
        def _():
            for h in range(heads):
                forward(h)

    last_queries()

    if depth > 0:
        @pl.when((block % 2 == 0) & (block < n_seq - 1))
        def _():
            for h in range(heads):
                forward(h)

    for n in aided:
        @pl.when(is_aided(n, block))
        def _():
            aid_copy(n).wait_send()

        @pl.when(is_aided(n, block - 1))
        def _():
            back_copy(n).wait_send()
    near_copy.wait_send()
    for c in range(len(pieces)):
        for j in range(n_pair - 1):
            if c in aided:
                @pl.when(jnp.logical_not(is_aided(c, block)))
                def _():
                    far_copy(j, c).wait_send()
            else:
                far_copy(j, c).wait_send()
            (relay_copy if c < relayed else cross_copy)(j, c).wait_send()

    @pl.when(block < n_seq - 1)
    def _():
        for h in range(heads):
            finish(h)

    @pl.when(block == n_seq - 1)
    def _():
        for h in range(heads):
            for level in range(depth):
                wait_level(h, level)
            finish(h)

    if depth > 0:
        @pl.when(block < n_seq - 1)
        def _():
            for h in range(heads):
                for u in range(CUTS):
                    up_copy(h, u, 0).wait_send()
            for level in range(1, depth):
                @pl.when((block // 2**level % 2 == 1) & (block % 2**level != 2**level - 1))
                def _():
                    for h in range(heads):
                        for u in range(CUTS):
                            pass_copy(h, u, level).wait_send()


def on_device(n_head, n_seq, tokens, q_weight, k_weight, v_weight, level_table, level_index, out_gain):
    rows, feats = tokens.shape
    total, width = q_weight.shape
    heads, quant = level_table.shape
    hd = width // heads
    depth = min(n_seq.bit_length() - 1, level_index.shape[0] - 1)
    pairs = n_head // 2
    far = max(pairs - 1, 1)
    n_chunk = len(SHARES)
    dma = pltpu.SemaphoreType.DMA
    anywhere = pl.BlockSpec(memory_space=pltpu.HBM)
    result = pl.pallas_call(
        functools.partial(fused, n_head, n_seq, depth),
        out_shape=pltpu.VMEM((rows, width), BF16),
        in_specs=[anywhere] * 7,
        out_specs=pl.BlockSpec(memory_space=pltpu.VMEM),
        scratch_shapes=[
            pltpu.VMEM((pairs, rows, 2 * feats), BF16),
            pltpu.VMEM((total, width), BF16),
            pltpu.VMEM((total, width), BF16),
            pltpu.VMEM((total, width), BF16),
            pltpu.VMEM((rows, width), F32),
            pltpu.VMEM((rows, width), F32),
            pltpu.VMEM((rows, width), F32),
            pltpu.VMEM((rows, width), F32),
            pltpu.VMEM((heads, rows, max(depth, 1) * hd), BF16),
            pltpu.VMEM((depth + 1, rows, width), F32),
            pltpu.VMEM((heads, hd, hd), F32),
            pltpu.VMEM((heads, max(depth, 1) * hd, hd), BF16),
            pltpu.VMEM((heads, hd, hd), BF16),
            pltpu.VMEM((rows, width), BF16),
            pltpu.VMEM((rows, width), BF16),
            pltpu.VMEM((len(GROUPS), heads, hd, hd), BF16),
            pltpu.VMEM((sum(row_chunks(rows)[n][1] for n in AIDED), feats), BF16),
            pltpu.VMEM(level_index.shape, jnp.int32),
            pltpu.VMEM((1, width), F32),
            pltpu.SMEM((heads, quant), F32),
            pltpu.VMEM((quant, width), F32),
            pltpu.VMEM((3 * quant, width), BF16),
            dma((7,)),
            dma((2,)),
            dma((far, n_chunk)),
            dma((far, n_chunk)),
            dma((pairs, 2, n_chunk)),
            dma((heads, CUTS)),
            dma((heads, max(depth, 1), CUTS)),
            dma((heads, max(depth, 1), CUTS)),
            dma((len(AIDED),)),
            dma((len(AIDED),)),
            dma((len(AIDED),)),
        ],
        compiler_params=pltpu.CompilerParams(
            collective_id=0, has_side_effects=True, vmem_limit_bytes=56 * 1024 * 1024
        ),
    )(tokens, q_weight, k_weight, v_weight, level_table, level_index, out_gain.reshape(1, width))
    return result


def solution(mesh):
    return jax.shard_map(
        functools.partial(on_device, mesh.shape["head"], mesh.shape["seq"]),
        mesh=mesh,
        in_specs=(
            P(("groups", "seq"), "head"),
            P(None, "head"),
            P(None, "head"),
            P(None, "head"),
            P("head", None),
            P(None, ("groups", "seq")),
            P("head"),
        ),
        out_specs=P(("groups", "seq"), "head"),
        check_vma=False,
    )
```

```python
import functools

import jax
import jax.numpy as jnp
from jax import lax
from jax.experimental import pallas as pl
from jax.experimental.pallas import tpu as pltpu
from jax.sharding import PartitionSpec as P

MESH = pl.DeviceIdType.MESH
F32 = jnp.float32
BF16 = jnp.bfloat16
EPS = 1e-06
SHARES = (16, 16, 9, 3, 4, 8, 6, 2)
CHUNKS = (1, 1, 3, 1, 2)
AIDED = (2, 3)
GROUPS = (1, 1, 1, 1, 1)
DUAL = 1
CUTS = 1


def row_chunks(rows):
    sizes = [rows // sum(SHARES) * part for part in SHARES]
    starts, at = [], 0
    for size in sizes:
        starts.append((at, size))
        at += size
    return starts


def fused(
    n_head, n_seq, depth,
    tok, wq_in, wk_in, wv_in, table_in, index_in, gain_in,
    out,
    gat, wq, wk, wv, acc_q, acc_k, acc_v, local, scaled_q, lev, state, merged, outbox,
    keys, vals, prior, guests,
    index, gain, table, wide, parts,
    load_sem, near_send, far_send, relay_send, recv_sem, up_send, pass_send, up_recv, aid_send, aid_recv, back_send,
):
    rows, feats = tok.shape
    width = wq_in.shape[1]
    heads, quant = table.shape
    hd = width // heads
    part_rows = hd // CUTS
    pieces = row_chunks(rows)
    relayed = len(pieces) - DUAL
    parts_of, spans, chunks, firsts = [], [], [], []
    for n in CHUNKS:
        first = sum(map(len, parts_of))
        parts_of.append(list(range(first, first + n)))
        chunks.append((pieces[first][0], sum(size for _, size in pieces[first:first + n])))
    for n in GROUPS:
        first = sum(GROUPS[:len(firsts)])
        firsts.append(first)
        spans.append((chunks[first][0], sum(chunks[first + n - 1])))
    me = lax.axis_index("head")
    block = lax.axis_index("seq")
    pair = me // 2
    side = me % 2
    partner = pair * 2 + 1 - side
    n_pair = n_head // 2
    far_pairs = [(pair + 1 + j) % n_pair for j in range(n_pair - 1)]
    aided = AIDED if n_pair == 2 and n_seq > 1 else ()

    def is_aided(n, b):
        if n == AIDED[0]:
            return (b >= 0) & (b < n_seq - 1)
        return b == n_seq - 2

    def cols_of(s):
        return pl.ds(pl.multiple_of(s * feats, feats), feats)

    def wrows(p):
        return pl.ds(pl.multiple_of(p * (2 * feats), 2 * feats), 2 * feats)

    def wpart(p, s):
        return pl.ds(pl.multiple_of((p * 2 + s) * feats, feats), feats)

    loads = [
        pltpu.make_async_copy(tok, gat.at[pair, :, cols_of(side)], load_sem.at[0]),
        pltpu.make_async_copy(wk_in, wk, load_sem.at[1]),
        pltpu.make_async_copy(wv_in, wv, load_sem.at[2]),
        pltpu.make_async_copy(wq_in, wq, load_sem.at[3]),
        pltpu.make_async_copy(index_in, index, load_sem.at[4]),
        pltpu.make_async_copy(gain_in, gain, load_sem.at[5]),
        pltpu.make_async_copy(table_in, table, load_sem.at[6]),
    ]
    barrier = pltpu.get_barrier_semaphore()
    for p in far_pairs:
        for s in (side, 1 - side)[:1 + min(DUAL, 1)]:
            pl.semaphore_signal(barrier, inc=1, device_id={"head": p * 2 + s}, device_id_type=MESH)
    pl.semaphore_signal(barrier, inc=1, device_id={"head": partner}, device_id_type=MESH)

    @pl.when(block > 0)
    def _():
        pl.semaphore_signal(barrier, inc=1, device_id={"seq": block - 1}, device_id_type=MESH)

    @pl.when(block < n_seq - 1)
    def _():
        pl.semaphore_signal(barrier, inc=1, device_id={"seq": block + 1}, device_id_type=MESH)

    if aided:
        for b in (block - 1, block + 1):
            @pl.when((b >= 0) & (b < n_seq))
            def _():
                pl.semaphore_signal(
                    barrier, inc=1, device_id={"head": far_pairs[0] * 2 + side, "seq": b}, device_id_type=MESH
                )

    for n in (6, 4, 5, 0, 1, 2, 3):
        loads[n].start()

    beside = (block + n_seq - 1) // n_seq + (2 * n_seq - 2 - block) // n_seq
    pl.semaphore_wait(barrier, 1 + (n_pair - 1) * (1 + min(DUAL, 1)) + beside * (2 if aided else 1))

    def piece(p, s, c):
        at, size = pieces[c]
        return gat.at[p, pl.ds(at, size), cols_of(s)]

    def far_copy(j, c):
        at, size = pieces[c]
        return pltpu.make_async_remote_copy(
            src_ref=tok.at[pl.ds(at, size), :], dst_ref=piece(pair, side, c),
            send_sem=far_send.at[j, c], recv_sem=recv_sem.at[pair, side, c],
            device_id={"head": far_pairs[j] * 2 + side}, device_id_type=MESH,
        )

    def cross_copy(j, c):
        at, size = pieces[c]
        return pltpu.make_async_remote_copy(
            src_ref=tok.at[pl.ds(at, size), :], dst_ref=piece(pair, side, c),
            send_sem=relay_send.at[j, c], recv_sem=recv_sem.at[pair, side, c],
            device_id={"head": far_pairs[j] * 2 + 1 - side}, device_id_type=MESH,
        )

    def spot(n):
        at = sum(pieces[a][1] for a in AIDED[:AIDED.index(n)])
        return guests.at[pl.ds(at, pieces[n][1]), :]

    def aid_copy(n):
        at, size = pieces[n]
        return pltpu.make_async_remote_copy(
            src_ref=tok.at[pl.ds(at, size), :], dst_ref=spot(n),
            send_sem=aid_send.at[AIDED.index(n)], recv_sem=aid_recv.at[AIDED.index(n)],
            device_id={"head": far_pairs[0] * 2 + side, "seq": block + 1}, device_id_type=MESH,
        )

    def back_copy(n):
        return pltpu.make_async_remote_copy(
            src_ref=spot(n), dst_ref=piece(far_pairs[0], side, n),
            send_sem=back_send.at[AIDED.index(n)], recv_sem=recv_sem.at[far_pairs[0], side, n],
            device_id={"seq": block - 1}, device_id_type=MESH,
        )

    near_copy = pltpu.make_async_remote_copy(
        src_ref=tok, dst_ref=gat.at[pair, :, cols_of(side)],
        send_sem=near_send.at[0], recv_sem=near_send.at[1],
        device_id={"head": partner}, device_id_type=MESH,
    )

    def relay_copy(j, c):
        p = far_pairs[j]
        return pltpu.make_async_remote_copy(
            src_ref=piece(p, side, c), dst_ref=piece(p, side, c),
            send_sem=relay_send.at[j, c], recv_sem=recv_sem.at[p, side, c],
            device_id={"head": partner}, device_id_type=MESH,
        )

    def arrived(p, s, c):
        here = piece(p, s, c)
        pltpu.make_async_remote_copy(
            src_ref=here, dst_ref=here, send_sem=near_send.at[0], recv_sem=recv_sem.at[p, s, c],
            device_id={"head": partner}, device_id_type=MESH,
        ).wait_recv()

    for n in aided:
        @pl.when(is_aided(n, block))
        def _():
            aid_copy(n).start()
    for c in range(len(pieces)):
        for j in range(n_pair - 1):
            if c in aided:
                @pl.when(jnp.logical_not(is_aided(c, block)))
                def _():
                    far_copy(j, c).start()
            else:
                far_copy(j, c).start()
            if c >= relayed:
                cross_copy(j, c).start()
        if c == 0:
            near_copy.start()

    for level in range(depth):
        @pl.when(block // 2**level % 2 == 0)
        def _():
            merged[:, level * hd:(level + 1) * hd, :] = jnp.zeros((heads, hd, hd), BF16)
    state[...] = jnp.zeros_like(state)

    loads[6].wait()
    for q in range(quant):
        for h in range(heads):
            wide[q:q + 1, h * hd:(h + 1) * hd] = jnp.full((1, hd), table[h, q], F32)
    top = wide[...].astype(BF16)
    rest = wide[...] - top.astype(F32)
    mid = rest.astype(BF16)
    low = (rest - mid.astype(F32)).astype(BF16)
    parts[...] = jnp.concatenate([top, mid, low], axis=0)
    loads[4].wait()
    loads[5].wait()

    step = min(rows, 256)
    for level in range(depth + 1):
        for at in range(0, rows, step):
            column = jnp.broadcast_to(index[level:level + 1, at:at + step], (3 * quant, step))
            ids = lax.broadcasted_iota(jnp.int32, (3 * quant, step), 0) % quant
            one_hot = jnp.where(column == ids, 1.0, 0.0).astype(BF16)
            lev[level, at:at + step, :] = lax.dot_general(
                one_hot, parts[...], (((0,), (0,)), ((), ())), preferred_element_type=F32
            )

    loads[0].wait()
    for copy in loads[1:4]:
        copy.wait()
    near_copy.wait_recv()
    for at in range(0, rows, step):
        here = gat[pair, at:at + step, :]
        for acc, w in ((acc_k, wk), (acc_v, wv), (acc_q, wq)):
            acc[at:at + step, :] = jnp.dot(here, w[wrows(pair), :], preferred_element_type=F32)

    def state_part(level, u):
        return pl.ds(level * hd + u * part_rows, part_rows)

    def up_copy(h, u, level):
        return pltpu.make_async_remote_copy(
            src_ref=outbox.at[h, pl.ds(u * part_rows, part_rows), :],
            dst_ref=merged.at[h, state_part(level, u), :],
            send_sem=up_send.at[h, u], recv_sem=up_recv.at[h, level, u],
            device_id={"seq": block + 1}, device_id_type=MESH,
        )

    def pass_copy(h, u, level):
        here = merged.at[h, state_part(level, u), :]
        return pltpu.make_async_remote_copy(
            src_ref=here, dst_ref=here,
            send_sem=pass_send.at[h, level, u], recv_sem=up_recv.at[h, level, u],
            device_id={"seq": block + 1}, device_id_type=MESH,
        )

    def add_far(total, here, w, p):
        return total + jnp.dot(here, w[wrows(p), :], preferred_element_type=F32)

    def take(c):
        for n in parts_of[c]:
            if n < relayed:
                for j, p in enumerate(far_pairs):
                    arrived(p, side, n)
                    relay_copy(j, n).start()

    def add_side(totals, c, s):
        at, size = chunks[c]
        for p in far_pairs:
            here = gat[p, at:at + size, cols_of(s)]
            totals = [
                total + jnp.dot(here, w[wpart(p, s), :], preferred_element_type=F32)
                for total, w in zip(totals, (wk, wv))
            ]
        return totals

    def keys_and_values(c):
        at, size = chunks[c]
        last = c == len(chunks) - 1
        totals = [acc_k[at:at + size, :], acc_v[at:at + size, :]]
        for n in parts_of[c]:
            if n >= relayed:
                for p in far_pairs:
                    arrived(p, side, n)
        if last:
            totals = add_side(totals, c, side)
        for n in parts_of[c]:
            for p in far_pairs:
                arrived(p, 1 - side, n)
        if last:
            totals = add_side(totals, c, 1 - side)
        else:
            for p in far_pairs:
                here = gat[p, at:at + size, :]
                totals = [add_far(total, here, w, p) for total, w in zip(totals, (wk, wv))]
        raw_k, raw_v = totals
        k_of, v_of = [], []
        for h in range(heads):
            cut = slice(h * hd, (h + 1) * hd)
            k = raw_k[:, cut]
            k_of.append((k * lax.rsqrt(jnp.sum(k * k, -1, keepdims=True) + EPS)).astype(BF16))
            v_of.append(raw_v[:, cut].astype(BF16))
        grown = [
            lax.dot_general(k, v, (((0,), (0,)), ((), ())), preferred_element_type=F32)
            for k, v in zip(k_of, v_of)
        ]
        for h in range(heads):
            cut = slice(h * hd, (h + 1) * hd)
            before = state[h]
            if c in firsts:
                prior[firsts.index(c), h] = before.astype(BF16)
            after = before + grown[h]
            state[h] = after
            if last:
                outbox[h] = after.astype(BF16)
        if last and depth > 0:
            @pl.when(block % 2 == 0)
            def _():
                for h in range(heads):
                    for u in range(CUTS):
                        up_copy(h, u, 0).start()
        for h in range(heads):
            cut = slice(h * hd, (h + 1) * hd)
            keys[at:at + size, cut] = k_of[h]
            vals[at:at + size, cut] = v_of[h]

    def queries(g):
        at, end = spans[g]
        size = end - at
        raw_q = acc_q[at:end, :]
        for p in far_pairs:
            raw_q = add_far(raw_q, gat[p, at:end, :], wq, p)
        cuts = [slice(h * hd, (h + 1) * hd) for h in range(heads)]
        own_of = []
        for h, cut in enumerate(cuts):
            q = raw_q[:, cut]
            q = q * lax.rsqrt(jnp.sum(q * q, -1, keepdims=True) + EPS)
            own_of.append((q * lev[0, at:end, cut]).astype(BF16))
            for level in range(depth):
                scaled_q[h, at:end, level * hd:(level + 1) * hd] = (
                    q * lev[level + 1, at:end, cut]
                ).astype(BF16)
        causal = lax.broadcasted_iota(jnp.int32, (size, size), 0) >= lax.broadcasted_iota(
            jnp.int32, (size, size), 1
        )
        scores_of = [
            lax.dot_general(
                own_of[h], keys[at:end, cut], (((1,), (1,)), ((), ())), preferred_element_type=F32
            )
            for h, cut in enumerate(cuts)
        ]
        scores_of = [jnp.where(causal, scores, 0.0).astype(BF16) for scores in scores_of]
        for h, cut in enumerate(cuts):
            local[at:end, cut] = jnp.dot(
                scores_of[h], vals[at:end, cut], preferred_element_type=F32
            ) + jnp.dot(own_of[h], prior[g, h], preferred_element_type=F32)

    for n in aided:
        @pl.when(is_aided(n, block - 1))
        def _():
            aid_copy(n).wait_recv()
            back_copy(n).start()
    take(0)
    for c in range(len(chunks)):
        if c + 1 < len(chunks):
            take(c + 1)
        keys_and_values(c)
        if c + 1 in firsts:
            queries(firsts.index(c + 1) - 1)

    def wait_level(h, level):
        @pl.when(block // 2**level % 2 == 1)
        def _():
            for u in range(CUTS):
                pass_copy(h, u, level).wait_recv()

    def forward(h):
        for level in range(depth):
            for u in range(CUTS):
                @pl.when(block // 2**level % 2 == 1)
                def _():
                    pass_copy(h, u, level).wait_recv()
                if level > 0:
                    @pl.when((block // 2**level % 2 == 1) & (block % 2**level != 2**level - 1))
                    def _():
                        pass_copy(h, u, level).start()

                    @pl.when(block % 2 ** (level + 1) == 2**level - 1)
                    def _():
                        mine = pl.ds(u * part_rows, part_rows)
                        total = state[h, mine, :]
                        for below in range(level):
                            total = total + merged[h, state_part(below, u), :].astype(F32)
                        outbox[h, mine, :] = total.astype(BF16)
                        up_copy(h, u, level).start()

    def last_queries():
        queries(len(spans) - 1)

    def finish(h):
        cut = slice(h * hd, (h + 1) * hd)
        tile = min(rows, 128)
        for at in range(0, rows, tile):
            both = local[at:at + tile, cut]
            if depth > 0:
                both = both + jnp.dot(
                    scaled_q[h, at:at + tile, :], merged[h], preferred_element_type=F32
                )
            scale = lax.rsqrt(jnp.sum(both * both, -1, keepdims=True) * (1.0 / hd) + EPS)
            out[at:at + tile, cut] = (both * scale * gain[:, cut]).astype(BF16)

    if depth > 0:
        @pl.when((block % 2 == 1) & (block < n_seq - 1))
        def _():
            for h in range(heads):
                forward(h)

    last_queries()

    if depth > 0:
        @pl.when((block % 2 == 0) & (block < n_seq - 1))
        def _():
            for h in range(heads):
                forward(h)

    for n in aided:
        @pl.when(is_aided(n, block))
        def _():
            aid_copy(n).wait_send()

        @pl.when(is_aided(n, block - 1))
        def _():
            back_copy(n).wait_send()
    near_copy.wait_send()
    for c in range(len(pieces)):
        for j in range(n_pair - 1):
            if c in aided:
                @pl.when(jnp.logical_not(is_aided(c, block)))
                def _():
                    far_copy(j, c).wait_send()
            else:
                far_copy(j, c).wait_send()
            (relay_copy if c < relayed else cross_copy)(j, c).wait_send()

    @pl.when(block < n_seq - 1)
    def _():
        for h in range(heads):
            finish(h)

    @pl.when(block == n_seq - 1)
    def _():
        for h in range(heads):
            for level in range(depth):
                if n_seq & (n_seq - 1) == 0:
                    for u in range(CUTS):
                        pass_copy(h, u, level).wait_recv()
                else:
                    wait_level(h, level)
            finish(h)

    if depth > 0:
        @pl.when(block < n_seq - 1)
        def _():
            for h in range(heads):
                for u in range(CUTS):
                    up_copy(h, u, 0).wait_send()
            for level in range(1, depth):
                @pl.when((block // 2**level % 2 == 1) & (block % 2**level != 2**level - 1))
                def _():
                    for h in range(heads):
                        for u in range(CUTS):
                            pass_copy(h, u, level).wait_send()


def on_device(n_head, n_seq, tokens, q_weight, k_weight, v_weight, level_table, level_index, out_gain):
    rows, feats = tokens.shape
    total, width = q_weight.shape
    heads, quant = level_table.shape
    hd = width // heads
    depth = min(n_seq.bit_length() - 1, level_index.shape[0] - 1)
    pairs = n_head // 2
    far = max(pairs - 1, 1)
    n_chunk = len(SHARES)
    dma = pltpu.SemaphoreType.DMA
    anywhere = pl.BlockSpec(memory_space=pltpu.HBM)
    result = pl.pallas_call(
        functools.partial(fused, n_head, n_seq, depth),
        out_shape=pltpu.VMEM((rows, width), BF16),
        in_specs=[anywhere] * 7,
        out_specs=pl.BlockSpec(memory_space=pltpu.VMEM),
        scratch_shapes=[
            pltpu.VMEM((pairs, rows, 2 * feats), BF16),
            pltpu.VMEM((total, width), BF16),
            pltpu.VMEM((total, width), BF16),
            pltpu.VMEM((total, width), BF16),
            pltpu.VMEM((rows, width), F32),
            pltpu.VMEM((rows, width), F32),
            pltpu.VMEM((rows, width), F32),
            pltpu.VMEM((rows, width), F32),
            pltpu.VMEM((heads, rows, max(depth, 1) * hd), BF16),
            pltpu.VMEM((depth + 1, rows, width), F32),
            pltpu.VMEM((heads, hd, hd), F32),
            pltpu.VMEM((heads, max(depth, 1) * hd, hd), BF16),
            pltpu.VMEM((heads, hd, hd), BF16),
            pltpu.VMEM((rows, width), BF16),
            pltpu.VMEM((rows, width), BF16),
            pltpu.VMEM((len(GROUPS), heads, hd, hd), BF16),
            pltpu.VMEM((sum(row_chunks(rows)[n][1] for n in AIDED), feats), BF16),
            pltpu.VMEM(level_index.shape, jnp.int32),
            pltpu.VMEM((1, width), F32),
            pltpu.SMEM((heads, quant), F32),
            pltpu.VMEM((quant, width), F32),
            pltpu.VMEM((3 * quant, width), BF16),
            dma((7,)),
            dma((2,)),
            dma((far, n_chunk)),
            dma((far, n_chunk)),
            dma((pairs, 2, n_chunk)),
            dma((heads, CUTS)),
            dma((heads, max(depth, 1), CUTS)),
            dma((heads, max(depth, 1), CUTS)),
            dma((len(AIDED),)),
            dma((len(AIDED),)),
            dma((len(AIDED),)),
        ],
        compiler_params=pltpu.CompilerParams(
            collective_id=0, has_side_effects=True, vmem_limit_bytes=56 * 1024 * 1024
        ),
    )(tokens, q_weight, k_weight, v_weight, level_table, level_index, out_gain.reshape(1, width))
    return result


def solution(mesh):
    return jax.shard_map(
        functools.partial(on_device, mesh.shape["head"], mesh.shape["seq"]),
        mesh=mesh,
        in_specs=(
            P(("groups", "seq"), "head"),
            P(None, "head"),
            P(None, "head"),
            P(None, "head"),
            P("head", None),
            P(None, ("groups", "seq")),
            P("head"),
        ),
        out_specs=P(("groups", "seq"), "head"),
        check_vma=False,
    )
```
